256 devices in a mesh: pole: 2 (over core), row: 4 (over y), col: 2 (over x_hi), layer: 16 (over z, x_lo).
Axes of the slice: x: 4 (x_hi: 2, x_lo: 2; x = x_hi * 2 + x_lo), y: 4, z: 8, core: 2. Of those that a mesh axis runs over, the one named last changes fastest.
Arguments:
- hamilton: bfloat16 [4096, 4096], P('layer', ('row', 'col')), may hold values from -0.0014648438 to 0.0014648438
- intersection: bfloat16 [4096, 4096], P('layer', ('row', 'col')), may hold values from -0.0014648438 to 0.0014648438
- guess: bfloat16 [2, 2, 4096, 4096], P('pole', None, 'layer', ('row', 'col')), may hold values from -6 to 6
- poles: float32 [2, 2], P('pole'), may hold values from -1.5 to 1.5
- weights: float32 [2, 2], P('pole'), may hold values from -1 to 1
- keep: int32 [2, 32, 32], P('pole'), may hold values from 0 to 1, as said below
Outputs:
- density: float32 [16, 2, 128, 4096], P('layer', 'pole', None, ('row', 'col'))
The draws below stay inside these ranges and needn't reach their ends.
Inputs may be any that keep to these rules, and one draw needn't show every extreme that they name: keep[p, i, j] is 1 where tile (i, j) survives pole p's filter and 0 where it is dropped; diagonal tiles are always kept.
All inputs are finite; a program needn't handle non-finite values.
Results may differ from the reference program's by a relative error of at most 0.0032.
Values may be sent and summed in bfloat16 or wider, within the bound.
No kernel may reach another device: no remote copies, remote signals or barrier semaphores. Data moves between devices by JAX's collectives and lax.ppermute only.
A program may use at most 64 MiB of HBM per device.

```python
import jax
import jax.numpy as jnp

ROWS_DEV = 256
BLOCK = 128
POLES = 2
ORDER = 4096
TILES = 32
N_POLE = 2
N_LAYER = 16


def draw_keep(key, part):
    first_key, second_key = jax.random.split(jax.random.fold_in(key, 17))
    level = jax.random.randint(first_key, (POLES, TILES, 1), 1, 8)
    coin = jax.random.randint(second_key, (POLES, TILES, TILES), 0, 8)
    diagonal = jnp.arange(TILES)[:, None] == jnp.arange(TILES)[None, :]
    return jnp.where((coin < level) | diagonal[None], 1, 0).astype(jnp.int32)


def block_levels(rng, extent, pieces, smallest, largest):
    loudness = 1.0
    for dim, shards_of in pieces:
        heights = jax.random.uniform(jax.random.fold_in(jax.random.fold_in(rng, 6), dim), (shards_of,), jnp.float32, smallest / len(pieces), largest / len(pieces))
        loudness = loudness * jnp.repeat(jnp.exp(heights), extent[dim] // shards_of).reshape((-1,) + (1,) * (len(extent) - 1 - dim))
    return loudness


def centred(stream_key, extent, width, limit, cuts=(), kind=jnp.bfloat16):
    factor_of = block_levels(stream_key, extent, cuts, -0.22, 0.18) if cuts else 1.0
    array = jax.random.normal(stream_key, extent, jnp.float32) * width * factor_of
    return jnp.minimum(jnp.maximum(array, -limit), limit).astype(kind)


def setup_inputs(seed: int = 0) -> dict:
    keys = jax.random.split(jax.random.key(seed), 7)
    hamilton = centred(keys[0], (ORDER, ORDER), (1.0 / ORDER), 0.0014648438, ((0, 16), (1, 8)))
    intersection = centred(keys[1], (ORDER, ORDER), (1.0 / ORDER), 0.0014648438, ((0, 16), (1, 8)))
    guess = centred(keys[2], (POLES, 2, ORDER, ORDER), 1.0, 6.0, ((0, 2), (2, 16), (3, 8)))
    poles = jnp.clip(jax.random.uniform(keys[3], (POLES, 2), jnp.float32, -1.5, 1.5) * block_levels(keys[3], (POLES, 2), ((0, 2),), -0.4, 0.0), -1.5, 1.5)
    weights = jnp.clip(jax.random.uniform(keys[4], (POLES, 2), jnp.float32, -1.0, 1.0) * block_levels(keys[4], (POLES, 2), ((0, 2),), -0.4, 0.0), -1.0, 1.0)
    keep = draw_keep(jax.random.fold_in(keys[6], 71), 0)
    return dict(hamilton=hamilton, intersection=intersection, guess=guess, poles=poles, weights=weights, keep=keep)


def widen(keep_pole):
    return jnp.repeat(jnp.repeat(keep_pole, BLOCK, axis=0), BLOCK, axis=1).astype(jnp.float32)


def complex_dot(left_re, left_im, right_re, right_im):
    real_part = jnp.dot(left_re, right_re, preferred_element_type=jnp.float32) - jnp.dot(left_im, right_im, preferred_element_type=jnp.float32)
    imag_part = jnp.dot(left_re, right_im, preferred_element_type=jnp.float32) + jnp.dot(left_im, right_re, preferred_element_type=jnp.float32)
    return real_part, imag_part


def reference(hamilton, intersection, guess, poles, weights, keep):
    ham_full = hamilton.astype(jnp.float32)
    ovl_full = intersection.astype(jnp.float32)
    density = jnp.zeros((ORDER, ORDER), jnp.float32)
    for index in range(POLES):
        system_re = (poles[index, 0] * ovl_full - ham_full).astype(jnp.bfloat16)
        system_im = (poles[index, 1] * ovl_full).astype(jnp.bfloat16)
        guess_re = guess[index, 0]
        guess_im = guess[index, 1]
        filter_mask = widen(keep[index])
        prod_re, prod_im = complex_dot(system_re, system_im, guess_re, guess_im)
        prod_re = (filter_mask * prod_re).astype(jnp.bfloat16)
        prod_im = (filter_mask * prod_im).astype(jnp.bfloat16)
        back_re, back_im = complex_dot(guess_re, guess_im, prod_re, prod_im)
        refined_re = filter_mask * (2.0 * guess_re.astype(jnp.float32) - back_re)
        refined_im = filter_mask * (2.0 * guess_im.astype(jnp.float32) - back_im)
        density = density + weights[index, 0] * refined_re - weights[index, 1] * refined_im
    return density.reshape(N_LAYER, N_POLE, ROWS_DEV // N_POLE, ORDER)
```

```python
import functools

import jax
import jax.numpy as jnp
from jax import lax
from jax.experimental import pallas as pl
from jax.experimental.pallas import tpu as pltpu
from jax.sharding import Mesh
from jax.sharding import PartitionSpec as P

BLOCK = 128
LAYER = ("z", "x_lo")
X = ("col", "x_lo")
STEPS = (0, 1, 7, 2, 6, 3, 5, 4)


def fetch(array, axis, count, offset):
    return lax.ppermute(array, axis, [(i, (i - offset) % count) for i in range(count)])


def line_gather(own):
    got = {0: own}
    up, down = own, own
    for step in range(1, 4):
        up = fetch(up, "z", 8, 1)
        down = fetch(down, "z", 8, -1)
        got[step], got[8 - step] = up, down
    half = own.shape[0] // 2
    got[4] = jnp.concatenate([fetch(up[:half], "z", 8, 1), fetch(down[half:], "z", 8, -1)])
    return got


def plane_gather(own, first, second):
    line = jnp.stack([own] + [fetch(own, first, 4, d) for d in (1, 2, 3)])
    ahead = fetch(line, second, 4, 1)
    behind = fetch(line, second, 4, -1)
    far_low = fetch(ahead[:2], second, 4, 1)
    far_high = fetch(behind[2:], second, 4, -1)
    return jnp.concatenate([line, ahead, far_low, far_high, behind])


def block_slot(place, step, half):
    z, y, x = place[0], place[1], place[2]
    span = (z + step) % 8
    dy = (span // 2 - y + 4) % 4
    dx = ((span % 2) * 2 + half - x + 4) % 4
    return dy, dx


def gathered_blocks(pieces, held, sems):
    copies = [pltpu.make_async_copy(piece, held.at[i], sems.at[i]) for i, piece in enumerate(pieces)]
    for copy in copies:
        copy.start()

    def ready(i):
        pltpu.make_async_copy(pieces[0], held.at[i], sems.at[i]).wait()

    return ready


def product_kernel(place, weights, keep, sys_re_a, sys_im_a, sys_re_b, sys_im_b, *rest):
    pieces, (out, acc_re, acc_im, held, sems) = rest[:16], rest[16:]
    ready = gathered_blocks(pieces, held, sems)
    x_lo = place[2] % 2
    dot = functools.partial(jnp.dot, preferred_element_type=jnp.float32)
    acc_re[...] = jnp.zeros_like(acc_re)
    acc_im[...] = jnp.zeros_like(acc_im)

    @pl.loop(0, 16)
    def _(i):
        ready(i)
        step, rel = place[3 + i // 2], i % 2
        lane = pl.multiple_of(((x_lo + rel) % 2) * 256, 256)
        re_parts, im_parts = [], []
        for half in range(2):
            dy, dx = block_slot(place, step, half)
            re_parts += [sys_re_a[dy * 4 + dx, :, pl.ds(lane, 256)], sys_re_b[dx * 4 + dy, :, pl.ds(lane, 256)]]
            im_parts += [sys_im_a[dy * 4 + dx, :, pl.ds(lane, 256)], sys_im_b[dx * 4 + dy, :, pl.ds(lane, 256)]]
        s_re, s_im = jnp.concatenate(re_parts), jnp.concatenate(im_parts)
        g_re, g_im = held[i, 0], held[i, 1]
        acc_re[...] += dot(s_re, g_re) - dot(s_im, g_im)
        acc_im[...] += dot(s_re, g_im) + dot(s_im, g_re)

    kappa = place[1] * 4 + place[2]
    for i in range(4):
        for j in range(2):
            mask = keep[place[0] * 4 + i, kappa * 2 + j].astype(jnp.float32)
            rows, cols = pl.ds(i * BLOCK, BLOCK), pl.ds(j * BLOCK, BLOCK)
            p_re, p_im = acc_re[rows, cols], acc_im[rows, cols]
            q_re = mask * (weights[0] * p_re - weights[1] * p_im)
            q_im = mask * (weights[0] * p_im + weights[1] * p_re)
            local = pl.ds((i % 2) * BLOCK, BLOCK)
            out[i // 2, 0, local, cols] = q_re.astype(jnp.bfloat16)
            out[i // 2, 1, local, cols] = (-q_im).astype(jnp.bfloat16)


def refine_kernel(place, weights, keep, g_re, g_im, own, other, *rest):
    pieces, (out, acc, held, sems) = rest[:16], rest[16:]
    ready = gathered_blocks(pieces, held, sems)
    x_lo = place[2] % 2
    dot = functools.partial(jnp.dot, preferred_element_type=jnp.float32)
    acc[...] = jnp.zeros_like(acc)

    @pl.loop(0, 16)
    def _(i):
        ready(i)
        step, side = place[3 + i // 2], i % 2
        lane = pl.multiple_of(side * 256, 256)
        re_parts, im_parts = [], []
        for half in range(2):
            dy, dx = block_slot(place, step, half)
            re_parts.append(g_re[dy * 4 + dx, :, pl.ds(lane, 256)])
            im_parts.append(g_im[dx * 4 + dy, :, pl.ds(lane, 256)])
        acc[...] += dot(jnp.concatenate(re_parts), held[i, 0]) + dot(jnp.concatenate(im_parts), held[i, 1])

    kappa = place[1] * 4 + place[2]
    for i in range(4):
        for j in range(2):
            mask = keep[place[0] * 4 + i, kappa * 2 + j].astype(jnp.float32)
            local, cols = pl.ds((i % 2) * BLOCK, BLOCK), pl.ds(j * BLOCK, BLOCK)
            mine = x_lo == i // 2
            own_re = jnp.where(mine, own[0, local, cols].astype(jnp.float32), other[0, local, cols].astype(jnp.float32))
            own_im = jnp.where(mine, own[1, local, cols].astype(jnp.float32), other[1, local, cols].astype(jnp.float32))
            twice = 2.0 * (weights[0] * own_re - weights[1] * own_im)
            out[i // 2, i % 2, :, cols] = mask * (twice - acc[pl.ds(i * BLOCK, BLOCK), cols])


def call(kernel, out_shape, scratch, flops, operands):
    smem = pl.BlockSpec(memory_space=pltpu.SMEM)
    vmem = pl.BlockSpec(memory_space=pltpu.VMEM)
    return pl.pallas_call(
        kernel,
        out_shape=out_shape,
        in_specs=[smem] * 3 + [vmem] * (len(operands) - 19) + [pl.BlockSpec(memory_space=pl.ANY)] * 16,
        out_specs=vmem,
        scratch_shapes=scratch + [pltpu.VMEM((16, 2, 256, 256), jnp.bfloat16), pltpu.SemaphoreType.DMA((16,))],
        cost_estimate=pl.CostEstimate(flops=flops, bytes_accessed=1 << 24, transcendentals=0),
    )(*operands)


def per_device(hamilton, intersection, guess, poles, weights, keep):
    pole, z = lax.axis_index("pole"), lax.axis_index("z")
    y, x_hi, x_lo = lax.axis_index("row"), lax.axis_index("col"), lax.axis_index("x_lo")
    place = jnp.stack([z, y, x_hi * 2 + x_lo, *STEPS]).astype(jnp.int32)
    w, keep = weights[0], keep[0]
    g = guess[0]

    own = lax.dynamic_slice_in_dim(g, x_lo * 256, 256, axis=2)
    other = fetch(lax.dynamic_slice_in_dim(g, (1 - x_lo) * 256, 256, axis=2), "x_lo", 2, 1)
    shared = jnp.where(pole == 0, hamilton, intersection)

    own_line = line_gather(own)
    shared_a = plane_gather(shared[:128], X, "row")
    shared_b = plane_gather(shared[128:], "row", X)
    other_line = line_gather(other)
    mine = jnp.stack([shared_a, shared_b])
    theirs = fetch(mine, "pole", 2, 1)
    ham = jnp.where(pole == 0, mine, theirs).astype(jnp.float32)
    ovl = jnp.where(pole == 0, theirs, mine).astype(jnp.float32)
    sys_re = (poles[0, 0] * ovl - ham).astype(jnp.bfloat16)
    sys_im = (poles[0, 1] * ovl).astype(jnp.bfloat16)

    g_re = plane_gather(g[0], X, "row")
    g_im = plane_gather(g[1], "row", X)

    pieces = [p for step in STEPS for p in (own_line[step], other_line[step])]
    product = call(
        product_kernel,
        jax.ShapeDtypeStruct((2, 2, 256, 256), jnp.bfloat16),
        [pltpu.VMEM((512, 256), jnp.float32)] * 2,
        1 << 32,
        [place, w, keep, sys_re[0], sys_im[0], sys_re[1], sys_im[1], *pieces],
    )
    lines = [line_gather(product[0]), line_gather(product[1])]
    pieces = [lines[side][step] for step in STEPS for side in range(2)]
    contrib = call(
        refine_kernel,
        jax.ShapeDtypeStruct((2, 2, 128, 256), jnp.float32),
        [pltpu.VMEM((512, 256), jnp.float32)],
        1 << 31,
        [place, w, keep, g_re, g_im, own, other, *pieces],
    )
    away = fetch(lax.dynamic_index_in_dim(contrib, 1 - pole, 1, keepdims=False), "pole", 2, 1)
    summed = lax.dynamic_index_in_dim(contrib, pole, 1, keepdims=False) + away
    left = lax.dynamic_index_in_dim(summed, x_lo, 0, keepdims=False)
    right = fetch(lax.dynamic_index_in_dim(summed, 1 - x_lo, 0, keepdims=False), "x_lo", 2, 1)
    density = jnp.concatenate([jnp.where(x_lo == 0, left, right), jnp.where(x_lo == 0, right, left)], axis=1)
    return density.reshape(1, 1, 128, 512)


def solution(mesh):
    split = Mesh(
        mesh.devices.reshape(mesh.shape["pole"], mesh.shape["row"], mesh.shape["col"], 8, 2),
        ("pole", "row", "col", "z", "x_lo"),
    )
    return jax.shard_map(
        per_device,
        mesh=split,
        in_specs=(
            P(LAYER, ("row", "col")),
            P(LAYER, ("row", "col")),
            P("pole", None, LAYER, ("row", "col")),
            P("pole", None),
            P("pole", None),
            P("pole", None, None),
        ),
        out_specs=P(LAYER, "pole", None, ("row", "col")),
        check_vma=False,
    )
```

```python
import functools

import jax
import jax.numpy as jnp
from jax import lax
from jax.experimental import pallas as pl
from jax.experimental.pallas import tpu as pltpu
from jax.sharding import Mesh
from jax.sharding import PartitionSpec as P

BLOCK = 128
LAYER = ("z", "x_lo")
ALL = ("pole", "row", "col", "z", "x_lo")
SIZES = (2, 4, 2, 8, 2)
STEPS = (0, 1, 7, 2, 6, 3, 5, 4)
PRE, MID = 5, 2
LAST = len(STEPS) - PRE


def moved(array, source):
    pairs = []
    for p in range(2):
        for y in range(4):
            for x in range(4):
                for z in range(8):
                    at = [((((q * 4 + b) * 2 + a // 2) * 8 + c) * 2 + a % 2) for q, b, a, c in ((p, y, x, z), source(p, y, x, z))]
                    pairs.append((at[1], at[0]))
    return lax.ppermute(array, ALL, pairs)


def along_z(array, offset):
    return moved(array, lambda p, y, x, z: (p, y, x, (z + offset) % 8))


def across_plane(array, ring, offset):
    def source(p, y, x, z):
        return (p, y, (x + offset) % 4, z) if (p == 0) == (ring == 1) else (p, (y + offset) % 4, x, z)

    return moved(array, source)


def other_core(array):
    return moved(array, lambda p, y, x, z: (1 - p, y, x, z))


def x_partner(array):
    return moved(array, lambda p, y, x, z: (p, y, x ^ 1, z))


def line_gather(own, last):
    got = {0: own}
    up, down = own, own
    for step in range(1, 4):
        up = along_z(up, 1)
        down = along_z(down, -1)
        got[step], got[8 - step] = up, down
    got[4] = along_z(up, 1) if last == "u" else along_z(down, -1)
    return got


def second_ring(line):
    ahead = across_plane(line, 2, 1)
    behind = across_plane(line, 2, 3)
    far = across_plane(ahead[:2], 2, 1), across_plane(behind[2:], 2, 3)
    return [line, ahead, *far, behind]


def block_offsets(place, span, half, core):
    dy = (span // 2 - place[1] + 4) % 4
    dx = ((span % 2) * 2 + half - place[2] + 4) % 4
    return jnp.where(core == 0, dy, dx), jnp.where(core == 0, dx, dy)


def copy_in(sources, target, sem, second, first):
    near, ahead, far_low, far_high, behind = sources
    for source, chosen, entry in (
        (near, second == 0, first),
        (ahead, second == 1, first),
        (far_low, jnp.logical_and(second == 2, first < 2), first),
        (far_high, jnp.logical_and(second == 2, first >= 2), first - 2),
        (behind, second == 3, first),
    ):

        @pl.when(chosen)
        def _():
            pltpu.make_async_copy(source.at[entry], target, sem).start()


DOT = functools.partial(jnp.dot, preferred_element_type=jnp.float32)


def add_products(out, before, s_re, s_im, pieces, x_lo):
    lanes = [pl.ds(pl.multiple_of(((x_lo + rel) % 2) * 256, 256), 256) for rel in range(2)]
    re, im = [s_re[:, lane] for lane in lanes], [s_im[:, lane] for lane in lanes]
    g = [[pieces[rel][part] for rel in range(2)] for part in range(2)]
    out[1] = before[1] + DOT(jnp.concatenate(re + im, axis=1), jnp.concatenate(g[1] + g[0]))
    out[0] = before[0] + DOT(jnp.concatenate(re + [-s for s in im], axis=1), jnp.concatenate(g[0] + g[1]))


def place_system(place, poles, source, count, second, core, system):
    @pl.loop(0, 4 * count)
    def _(k):
        entry, part = k // 4, k % 4
        along, across = (entry % 4, second + entry // 4) if count != 2 else (entry + second[1], second[0])
        y = (place[1] + jnp.where(core == 0, across, along)) % 4
        x = (place[2] + jnp.where(core == 0, along, across)) % 4
        step = (y * 2 + x // 2 - place[0] + 8) % 8
        slot = jnp.where(step > 4, 2 * (8 - step), jnp.maximum(2 * step - 1, 0))
        rows = pl.ds(pl.multiple_of(((x % 2) * 2 + core) * 128 + part * 32, 32), 32)
        local = pl.ds(pl.multiple_of(part * 32, 32), 32)
        ham, ovl = [source[entry, kind, local].astype(jnp.float32) for kind in range(2)]
        system[slot, 0, rows] = (poles[0] * ovl - ham).astype(jnp.bfloat16)
        system[slot, 1, rows] = (poles[1] * ovl).astype(jnp.bfloat16)


def product_near(place, poles, near, ahead, far_low, far_high, behind, partner, system):
    for source, count, second in ((near, 4, 0), (ahead, 4, 1), (far_low, 2, (2, 0)), (far_high, 2, (2, 2)), (behind, 4, 3)):
        place_system(place, poles, source, count, second, place[3], system)
    place_system(place, poles, partner, 4, 0, 1 - place[3], system)


def product_pre(place, poles, before, far, *rest):
    pieces, (acc, system, held, sems) = rest[: 2 * PRE], rest[2 * PRE :]
    for i in range(PRE):
        for rel in range(2):
            pltpu.make_async_copy(pieces[2 * i + rel], held.at[i, rel], sems.at[i]).start()
    place_system(place, poles, far, 12, 1, 1 - place[3], system)
    acc[...] = jnp.zeros_like(acc)

    @pl.loop(0, PRE)
    def _(i):
        pltpu.make_async_copy(held.at[i], held.at[i], sems.at[i]).wait()
        add_products(acc, acc, system.at[i, 0], system.at[i, 1], held.at[i], place[2] % 2)


def product_mid(place, before, system, *rest):
    pieces, out = rest[:-1], rest[-1]
    for k in range(MID):
        add_products(out, before if k == 0 else out, system.at[PRE + k, 0], system.at[PRE + k, 1], pieces[2 * k : 2 * k + 2], place[2] % 2)


def product_late(place, weights, keep, before, system, *rest):
    pieces, outs, acc = rest[:2], rest[2:4], rest[4]
    add_products(acc, before, system.at[PRE + MID, 0], system.at[PRE + MID, 1], pieces, place[2] % 2)
    kappa = place[1] * 4 + place[2]
    for i in range(4):
        for j in range(2):
            mask = keep[place[0] * 4 + i, kappa * 2 + j].astype(jnp.float32)
            rows, cols = pl.ds(i * BLOCK, BLOCK), pl.ds(j * BLOCK, BLOCK)
            p_re, p_im = acc[0, rows, cols], acc[1, rows, cols]
            q_re = mask * (weights[0] * p_re - weights[1] * p_im)
            q_im = mask * (weights[0] * p_im + weights[1] * p_re)
            local = pl.ds((i % 2) * BLOCK, BLOCK)
            outs[i // 2][0, local, cols] = q_re.astype(jnp.bfloat16)
            outs[i // 2][1, local, cols] = (-q_im).astype(jnp.bfloat16)


def refined_sum(left, pieces):
    lhs = jnp.concatenate([left[:, part].reshape(512, 512) for part in range(2)], axis=1)
    return DOT(lhs, jnp.concatenate([pieces[side][part] for part in range(2) for side in range(2)]))


def refine_pre(place, *rest):
    lines, pieces = rest[:5], rest[5 : 5 + 2 * PRE]
    acc, late, held, left, sems = rest[5 + 2 * PRE :]
    pole = place[3]
    for i, step in enumerate(STEPS):
        span = (place[0] + step) % 8
        for side in range(2 if i < PRE else 0):
            pltpu.make_async_copy(pieces[2 * i + side], held.at[i, side], sems.at[i, 0]).start()
        for half in range(2):
            second, first = block_offsets(place, span, half, pole)
            target = left.at[i, half] if i < PRE else late.at[i - PRE, half]
            copy_in(lines, target, sems.at[i, 1], second, first)
    acc[...] = jnp.zeros_like(acc)

    @pl.loop(0, PRE)
    def _(i):
        pltpu.make_async_copy(left.at[i], left.at[i], sems.at[i, 1]).wait()
        pltpu.make_async_copy(held.at[i], held.at[i], sems.at[i, 0]).wait()
        acc[...] += refined_sum(left.at[i], held.at[i])

    @pl.loop(0, LAST)
    def _(i):
        pltpu.make_async_copy(late.at[i], late.at[i], sems.at[i + PRE, 1]).wait()


def refine_mid(before, late, *rest):
    pieces, out = rest[:-1], rest[-1]
    for k in range(MID):
        out[...] = (before if k == 0 else out)[...] + refined_sum(late.at[k], pieces[2 * k : 2 * k + 2])


def refine_late(place, weights, keep, before, late, own, other, *rest):
    pieces, kept, away, acc = rest[:2], rest[2], rest[3], rest[4]
    acc[...] = before[...] + refined_sum(late.at[MID], pieces)
    x_lo, kappa = place[2] % 2, place[1] * 4 + place[2]
    for slot, g in enumerate((own, other)):
        for out, core in ((kept, place[3]), (away, 1 - place[3])):
            tile = ((x_lo + slot) % 2) * 2 + core
            for j in range(2):
                mask = keep[place[0] * 4 + tile, kappa * 2 + j].astype(jnp.float32)
                cols, local = pl.ds(j * BLOCK, BLOCK), pl.ds(pl.multiple_of(core * BLOCK, BLOCK), BLOCK)
                own_re, own_im = [g[part, local, cols].astype(jnp.float32) for part in range(2)]
                twice = 2.0 * (weights[0] * own_re - weights[1] * own_im)
                out[slot, :, cols] = mask * (twice - acc[pl.ds(pl.multiple_of(tile * BLOCK, BLOCK), BLOCK), cols])


def call(kernel, outs, share, scalars=(), anywhere=(), vectors=(), scratch=(), room=10, aliases={}):
    smem, vmem = [pl.BlockSpec(memory_space=space) for space in (pltpu.SMEM, pltpu.VMEM)]
    return pl.pallas_call(
        kernel,
        out_shape=[jax.ShapeDtypeStruct(*out) for out in outs],
        in_specs=[smem] * len(scalars) + [pl.BlockSpec(memory_space=pl.ANY)] * len(anywhere) + [vmem] * len(vectors),
        out_specs=[vmem] * len(outs),
        scratch_shapes=scratch,
        input_output_aliases=aliases,
        compiler_params=pltpu.CompilerParams(vmem_limit_bytes=room << 20),
        cost_estimate=pl.CostEstimate(flops=share << 29, bytes_accessed=share << 21, transcendentals=0),
    )(*scalars, *anywhere, *vectors)


def per_device(hamilton, intersection, guess, poles, weights, keep):
    pole, z = lax.axis_index("pole"), lax.axis_index("z")
    y, x_hi, x_lo = lax.axis_index("row"), lax.axis_index("col"), lax.axis_index("x_lo")
    place = jnp.stack([z, y, x_hi * 2 + x_lo, pole]).astype(jnp.int32)
    w, keep, g = weights[0], keep[0], guess[0]
    f32, bf16 = jnp.float32, jnp.bfloat16

    shared = jnp.stack([lax.dynamic_slice_in_dim(a, pole * 128, 128, axis=0) for a in (hamilton, intersection)])
    ring = [shared] + [across_plane(shared, 1, d) for d in (1, 2, 3)]
    line = jnp.stack(ring)
    own = lax.dynamic_slice_in_dim(g, x_lo * 256, 256, axis=2)
    other = x_partner(lax.dynamic_slice_in_dim(g, (1 - x_lo) * 256, 256, axis=2))
    near = second_ring(line)
    far = [other_core(line), other_core(jnp.concatenate(near[1:]))]
    chains = (line_gather(own, "u"), line_gather(other, "d"))
    pieces = [chain[step] for step in STEPS for chain in chains]
    ahead, behind = across_plane(g, 1, 1), across_plane(g, 1, 3)
    far_low, far_high = across_plane(ahead[:1], 1, 1), across_plane(behind[1:], 1, 3)
    guess_line = jnp.stack([g, ahead, jnp.concatenate([far_low, far_high]), behind])
    guess_lines = second_ring(guess_line)

    system_shape = ((8, 2, 512, 512), bf16)
    (system,) = call(product_near, [system_shape], 2, [place, poles[0]], (), near + far[:1], room=16)
    acc, system = call(
        product_pre,
        [((2, 512, 256), f32), system_shape],
        PRE,
        [place, poles[0]],
        (),
        [system, far[1]] + pieces[: 2 * PRE],
        scratch=[pltpu.VMEM((PRE, 2, 2, 256, 256), bf16), pltpu.SemaphoreType.DMA((PRE,))],
        room=24,
        aliases={2: 1},
    )
    (acc,) = call(product_mid, [((2, 512, 256), f32)], MID, [place], (), [acc, system, *pieces[2 * PRE : -2]])
    upper, lower = call(
        product_late,
        [((2, 256, 256), bf16)] * 2,
        1,
        [place, w, keep],
        (),
        [acc, system, *pieces[-2:]],
        [pltpu.VMEM((2, 512, 256), f32)],
    )
    chains = (line_gather(upper, "u"), line_gather(lower, "d"))
    pieces = [chain[step] for step in STEPS for chain in chains]
    acc, left = call(
        refine_pre,
        [((512, 256), f32), ((LAST, 2, 2, 256, 512), bf16)],
        PRE,
        [place],
        (),
        guess_lines + pieces[: 2 * PRE],
        scratch=[
            pltpu.VMEM((PRE, 2, 2, 256, 256), bf16),
            pltpu.VMEM((PRE, 2, 2, 256, 512), bf16),
            pltpu.SemaphoreType.DMA((8, 2)),
        ],
        room=32,
    )
    (acc,) = call(refine_mid, [((512, 256), f32)], MID, (), (), [acc, left, *pieces[2 * PRE : -2]])
    kept, away = call(
        refine_late,
        [((2, 128, 256), f32)] * 2,
        1,
        [place, w, keep],
        (),
        [acc, left, own, other, *pieces[-2:]],
        [pltpu.VMEM((512, 256), f32)],
    )
    summed = kept + other_core(away)
    mine, theirs = summed[0], x_partner(summed[1])
    density = jnp.concatenate([jnp.where(x_lo == 0, mine, theirs), jnp.where(x_lo == 0, theirs, mine)], axis=1)
    return density.reshape(1, 1, 128, 512)


def solution(mesh):
    split = Mesh(mesh.devices.reshape(SIZES), ALL)
    return jax.shard_map(
        per_device,
        mesh=split,
        in_specs=(
            P(LAYER, ("row", "col")),
            P(LAYER, ("row", "col")),
            P("pole", None, LAYER, ("row", "col")),
            P("pole", None),
            P("pole", None),
            P("pole", None, None),
        ),
        out_specs=P(LAYER, "pole", None, ("row", "col")),
        check_vma=False,
    )
```

```python
import functools

import jax
import jax.numpy as jnp
from jax import lax
from jax.experimental import pallas as pl
from jax.experimental.pallas import tpu as pltpu
from jax.sharding import Mesh
from jax.sharding import PartitionSpec as P

BLOCK = 128
LAYER = ("z", "x_lo")
ALL = ("pole", "row", "col", "z", "x_lo")
SIZES = (2, 4, 2, 8, 2)
STEPS = (0, 1, 7, 2, 6, 3, 5, 4)
PRE, MID = 5, 2


def moved(array, source):
    pairs = []
    for p in range(2):
        for y in range(4):
            for x in range(4):
                for z in range(8):
                    at = [((((q * 4 + b) * 2 + a // 2) * 8 + c) * 2 + a % 2) for q, b, a, c in ((p, y, x, z), source(p, y, x, z))]
                    pairs.append((at[1], at[0]))
    return lax.ppermute(array, ALL, pairs)


def along_z(array, offset):
    return moved(array, lambda p, y, x, z: (p, y, x, (z + offset) % 8))


def across_plane(array, ring, offset):
    def source(p, y, x, z):
        return (p, y, (x + offset) % 4, z) if (p == 0) == (ring == 1) else (p, (y + offset) % 4, x, z)

    return moved(array, source)


def other_core(array):
    return moved(array, lambda p, y, x, z: (1 - p, y, x, z))


def x_partner(array):
    return moved(array, lambda p, y, x, z: (p, y, x ^ 1, z))


def line_gather(own, last):
    got = {0: own}
    up, down = own, own
    for step in range(1, 4):
        up = along_z(up, 1)
        down = along_z(down, -1)
        got[step], got[8 - step] = up, down
    got[4] = along_z(up, 1) if last == "u" else along_z(down, -1)
    return got


def second_ring(line):
    ahead = across_plane(line, 2, 1)
    behind = across_plane(line, 2, 3)
    return [line, ahead, across_plane(ahead, 2, 1), behind]


def block_offsets(place, span, half, core):
    dy = (span // 2 - place[1] + 4) % 4
    dx = ((span % 2) * 2 + half - place[2] + 4) % 4
    return jnp.where(core == 0, dy, dx), jnp.where(core == 0, dx, dy)


DOT = functools.partial(jnp.dot, preferred_element_type=jnp.float32)


def add_products(out, before, s_re, s_im, pieces, x_lo):
    lanes = [pl.ds(pl.multiple_of(((x_lo + rel) % 2) * 256, 256), 256) for rel in range(2)]
    re, im = [s_re[:, lane] for lane in lanes], [s_im[:, lane] for lane in lanes]
    g = [[pieces[rel][part] for rel in range(2)] for part in range(2)]
    out[1] = before[1] + DOT(jnp.concatenate(re + im, axis=1), jnp.concatenate(g[1] + g[0]))
    out[0] = before[0] + DOT(jnp.concatenate(re + [-s for s in im], axis=1), jnp.concatenate(g[0] + g[1]))


def place_system(place, poles, source, lines, core, system):
    @pl.loop(0, 16 * len(lines))
    def _(k):
        entry, along, part = k // 4, k // 4 % 4, k % 4
        across = sum(jnp.where(k // 16 == n, second, 0) for n, second in enumerate(lines))
        y = (place[1] + jnp.where(core == 0, across, along)) % 4
        x = (place[2] + jnp.where(core == 0, along, across)) % 4
        step = (y * 2 + x // 2 - place[0] + 8) % 8
        slot = jnp.where(step > 4, 2 * (8 - step), jnp.maximum(2 * step - 1, 0))
        rows = pl.ds(pl.multiple_of(((x % 2) * 2 + core) * 128 + part * 32, 32), 32)
        local = pl.ds(pl.multiple_of(part * 32, 32), 32)
        ham, ovl = [source[entry, kind, local].astype(jnp.float32) for kind in range(2)]
        system[slot, 0, rows] = (poles[0] * ovl - ham).astype(jnp.bfloat16)
        system[slot, 1, rows] = (poles[1] * ovl).astype(jnp.bfloat16)


def product_near(place, poles, near, ahead, behind, system, joined, sems):
    copies = []
    for k, source in enumerate((near, ahead, behind)):
        copies.append(pltpu.make_async_copy(source, joined.at[4 * k : 4 * k + 4], sems.at[k]))
        copies[k].start()
    for source, second in ((near, 0), (ahead, 1), (behind, 3)):
        place_system(place, poles, source, (second,), place[3], system)
    for copy in copies:
        copy.wait()


def product_far(place, poles, before, opposite, partner, system):
    place_system(place, poles, opposite, (2,), place[3], system)
    place_system(place, poles, partner, (0, 1, 3), 1 - place[3], system)


def product_all(place, poles, weights, keep, before, partner, *rest):
    pieces, (upper, lower, system, held, acc, sems) = rest[:16], rest[16:]
    for i in range(8):
        for rel in range(2):
            pltpu.make_async_copy(pieces[2 * i + rel], held.at[i, rel], sems.at[i]).start()
    place_system(place, poles, partner, (2,), 1 - place[3], system)
    acc[...] = jnp.zeros_like(acc)

    @pl.loop(0, 8)
    def _(i):
        pltpu.make_async_copy(held.at[i], held.at[i], sems.at[i]).wait()
        add_products(acc, acc, system.at[i, 0], system.at[i, 1], held.at[i], place[2] % 2)

    kappa = place[1] * 4 + place[2]
    for i in range(4):
        out, local = (upper, lower)[i // 2], pl.ds((i % 2) * BLOCK, BLOCK)
        for j in range(2):
            mask = keep[place[0] * 4 + i, kappa * 2 + j].astype(jnp.float32)
            rows, cols = pl.ds(i * BLOCK, BLOCK), pl.ds(j * BLOCK, BLOCK)
            p_re, p_im = acc[0, rows, cols], acc[1, rows, cols]
            q_re = mask * (weights[0] * p_re - weights[1] * p_im)
            q_im = mask * (weights[0] * p_im + weights[1] * p_re)
            out[0, local, cols] = q_re.astype(jnp.bfloat16)
            out[1, local, cols] = (-q_im).astype(jnp.bfloat16)


def refined_sum(left, pieces):
    lhs = jnp.concatenate([left[:, part].reshape(512, 512) for part in range(2)], axis=1)
    return DOT(lhs, jnp.concatenate([pieces[side][part] for part in range(2) for side in range(2)]))


def refine_pre(place, *rest):
    lines, pieces = rest[:4], rest[4 : 4 + 2 * PRE]
    acc, left, held, sems = rest[4 + 2 * PRE :]
    for i in range(PRE):
        for side in range(2):
            pltpu.make_async_copy(pieces[2 * i + side], held.at[i, side], sems.at[i, 0]).start()

    @pl.loop(0, 16)
    def _(k):
        i, half = k // 2, k % 2
        step = jnp.where(i % 2 == 1, (i + 1) // 2, (8 - i // 2) % 8)
        second, first = block_offsets(place, (place[0] + step) % 8, half, place[3])
        for n, line in enumerate(lines):

            @pl.when(second == n)
            def _():
                pltpu.make_async_copy(line.at[first], left.at[i, half], sems.at[i, 1]).start()

    acc[...] = jnp.zeros_like(acc)

    @pl.loop(0, PRE)
    def _(i):
        pltpu.make_async_copy(left.at[i], left.at[i], sems.at[i, 1]).wait()
        pltpu.make_async_copy(held.at[i], held.at[i], sems.at[i, 0]).wait()
        acc[...] += refined_sum(left.at[i], held.at[i])

    @pl.loop(PRE, 8)
    def _(i):
        pltpu.make_async_copy(left.at[i], left.at[i], sems.at[i, 1]).wait()


def refine_mid(before, left, *rest):
    pieces, out = rest[:-1], rest[-1]
    for k in range(MID):
        out[...] = (before if k == 0 else out)[...] + refined_sum(left.at[PRE + k], pieces[2 * k : 2 * k + 2])


def refine_late(place, weights, keep, before, left, own, other, *rest):
    pieces, kept, away, acc = rest[:2], rest[2], rest[3], rest[4]
    acc[...] = before[...] + refined_sum(left.at[PRE + MID], pieces)
    x_lo, kappa = place[2] % 2, place[1] * 4 + place[2]
    for slot, g in enumerate((own, other)):
        for out, core in ((kept, place[3]), (away, 1 - place[3])):
            tile = ((x_lo + slot) % 2) * 2 + core
            for j in range(2):
                mask = keep[place[0] * 4 + tile, kappa * 2 + j].astype(jnp.float32)
                cols, local = pl.ds(j * BLOCK, BLOCK), pl.ds(pl.multiple_of(core * BLOCK, BLOCK), BLOCK)
                own_re, own_im = [g[part, local, cols].astype(jnp.float32) for part in range(2)]
                twice = 2.0 * (weights[0] * own_re - weights[1] * own_im)
                out[slot, :, cols] = mask * (twice - acc[pl.ds(pl.multiple_of(tile * BLOCK, BLOCK), BLOCK), cols])


def call(kernel, outs, share, scalars=(), anywhere=(), vectors=(), scratch=(), room=10, aliases={}):
    smem, vmem = [pl.BlockSpec(memory_space=space) for space in (pltpu.SMEM, pltpu.VMEM)]
    return pl.pallas_call(
        kernel,
        out_shape=[jax.ShapeDtypeStruct(*out) for out in outs],
        in_specs=[smem] * len(scalars) + [pl.BlockSpec(memory_space=pl.ANY)] * len(anywhere) + [vmem] * len(vectors),
        out_specs=[vmem] * len(outs),
        scratch_shapes=scratch,
        input_output_aliases=aliases,
        compiler_params=pltpu.CompilerParams(vmem_limit_bytes=room << 20),
        cost_estimate=pl.CostEstimate(flops=share << 29, bytes_accessed=share << 21, transcendentals=0),
    )(*scalars, *anywhere, *vectors)


def per_device(hamilton, intersection, guess, poles, weights, keep):
    pole, z = lax.axis_index("pole"), lax.axis_index("z")
    y, x_hi, x_lo = lax.axis_index("row"), lax.axis_index("col"), lax.axis_index("x_lo")
    place = jnp.stack([z, y, x_hi * 2 + x_lo, pole]).astype(jnp.int32)
    w, keep, g = weights[0], keep[0], guess[0]
    f32, bf16 = jnp.float32, jnp.bfloat16

    shared = jnp.stack([lax.dynamic_slice_in_dim(a, pole * 128, 128, axis=0) for a in (hamilton, intersection)])
    ring = [shared] + [across_plane(shared, 1, d) for d in (1, 2, 3)]
    line = jnp.stack(ring)
    own = lax.dynamic_slice_in_dim(g, x_lo * 256, 256, axis=2)
    other = x_partner(lax.dynamic_slice_in_dim(g, (1 - x_lo) * 256, 256, axis=2))
    near = second_ring(line)
    chains = (line_gather(own, "u"), line_gather(other, "d"))
    pieces = [chain[step] for step in STEPS for chain in chains]
    guess_line = jnp.stack([g] + [across_plane(g, 1, d) for d in (1, 2, 3)])
    guess_lines = second_ring(guess_line)

    system_shape, at = ((8, 2, 512, 512), bf16), [place, poles[0]]
    system, joined = call(
        product_near,
        [system_shape, ((12, 2, 128, 512), bf16)],
        1,
        at,
        (),
        [near[0], near[1], near[3]],
        [pltpu.SemaphoreType.DMA((3,))],
    )
    far = [other_core(joined), other_core(near[2])]
    (system,) = call(product_far, [system_shape], 1, at, (), [system, near[2], far[0]], aliases={2: 0})
    upper, lower, _ = call(
        product_all,
        [((2, 256, 256), bf16)] * 2 + [system_shape],
        8,
        [*at, w, keep],
        (),
        [system, far[1]] + pieces,
        [pltpu.VMEM((8, 2, 2, 256, 256), bf16), pltpu.VMEM((2, 512, 256), f32), pltpu.SemaphoreType.DMA((8,))],
        room=14,
        aliases={4: 2},
    )
    chains = (line_gather(upper, "u"), line_gather(lower, "d"))
    pieces = [chain[step] for step in STEPS for chain in chains]
    acc, left = call(
        refine_pre,
        [((512, 256), f32), ((8, 2, 2, 256, 512), bf16)],
        PRE,
        [place],
        (),
        guess_lines + pieces[: 2 * PRE],
        scratch=[
            pltpu.VMEM((PRE, 2, 2, 256, 256), bf16),
            pltpu.SemaphoreType.DMA((8, 2)),
        ],
        room=16,
    )
    (acc,) = call(refine_mid, [((512, 256), f32)], MID, (), (), [acc, left, *pieces[2 * PRE : -2]])
    kept, away = call(
        refine_late,
        [((2, 128, 256), f32)] * 2,
        1,
        [place, w, keep],
        (),
        [acc, left, own, other, *pieces[-2:]],
        [pltpu.VMEM((512, 256), f32)],
    )
    summed = kept + other_core(away)
    mine, theirs = summed[0], x_partner(summed[1])
    density = jnp.concatenate([jnp.where(x_lo == 0, mine, theirs), jnp.where(x_lo == 0, theirs, mine)], axis=1)
    return density.reshape(1, 1, 128, 512)


def solution(mesh):
    split = Mesh(mesh.devices.reshape(SIZES), ALL)
    return jax.shard_map(
        per_device,
        mesh=split,
        in_specs=(
            P(LAYER, ("row", "col")),
            P(LAYER, ("row", "col")),
            P("pole", None, LAYER, ("row", "col")),
            P("pole", None),
            P("pole", None),
            P("pole", None, None),
        ),
        out_specs=P(LAYER, "pole", None, ("row", "col")),
        check_vma=False,
    )
```

```python
import functools

import jax
import jax.numpy as jnp
from jax import lax
from jax.experimental import pallas as pl
from jax.experimental.pallas import tpu as pltpu
from jax.sharding import Mesh
from jax.sharding import PartitionSpec as P

BLOCK = 128
LAYER = ("z", "x_lo")
ALL = ("pole", "row", "col", "z", "x_lo")
SIZES = (2, 4, 2, 8, 2)
STEPS = (0, 1, 7, 2, 6, 3, 5, 4)
PRE = 7


def moved(array, source):
    pairs = []
    for p in range(2):
        for y in range(4):
            for x in range(4):
                for z in range(8):
                    at = [((((q * 4 + b) * 2 + a // 2) * 8 + c) * 2 + a % 2) for q, b, a, c in ((p, y, x, z), source(p, y, x, z))]
                    pairs.append((at[1], at[0]))
    return lax.ppermute(array, ALL, pairs)


def along_z(array, offset):
    return moved(array, lambda p, y, x, z: (p, y, x, (z + offset) % 8))


def across_plane(array, ring, offset):
    def source(p, y, x, z):
        return (p, y, (x + offset) % 4, z) if (p == 0) == (ring == 1) else (p, (y + offset) % 4, x, z)

    return moved(array, source)


def other_core(array):
    return moved(array, lambda p, y, x, z: (1 - p, y, x, z))


def x_partner(array):
    return moved(array, lambda p, y, x, z: (p, y, x ^ 1, z))


def line_gather(own, last):
    got = {0: own}
    up, down = own, own
    for step in range(1, 4):
        up = along_z(up, 1)
        down = along_z(down, -1)
        got[step], got[8 - step] = up, down
    got[4] = along_z(up, 1) if last == "u" else along_z(down, -1)
    return got


def second_ring(line):
    ahead = across_plane(line, 2, 1)
    behind = across_plane(line, 2, 3)
    return [line, ahead, across_plane(ahead, 2, 1), behind]


def block_offsets(place, span, half, core):
    dy = (span // 2 - place[1] + 4) % 4
    dx = ((span % 2) * 2 + half - place[2] + 4) % 4
    return jnp.where(core == 0, dy, dx), jnp.where(core == 0, dx, dy)


DOT = functools.partial(jnp.dot, preferred_element_type=jnp.float32)


def half_product(side, place, poles, weights, keep, blocks, ready, held, out, acc):
    x_lo, cols = place[2] % 2, slice(side * BLOCK, side * BLOCK + BLOCK)
    lanes = [pl.ds(pl.multiple_of(((x_lo + rel) % 2) * 256, 256), 256) for rel in range(2)]
    acc[...] = jnp.zeros_like(acc)

    @pl.loop(0, 8)
    def _(i):
        ready(i)
        lhs = jnp.concatenate([jnp.concatenate([blocks[i, kind, :, lane] for kind in range(2)]) for lane in lanes], axis=1)
        rhs = [jnp.concatenate([held[i, rel, part, :, cols] for part in range(2)], axis=1) for rel in range(2)]
        acc[...] += DOT(lhs, jnp.concatenate(rhs))

    @pl.loop(0, 4)
    def _(i):
        mask = keep[place[0] * 4 + i, (place[1] * 4 + place[2]) * 2 + side].astype(jnp.float32)
        rows, ovl = [pl.ds(pl.multiple_of(start + i * BLOCK, BLOCK), BLOCK) for start in (0, 512)]
        p_re = poles[0] * acc[ovl, :BLOCK] - acc[rows, :BLOCK] - poles[1] * acc[ovl, BLOCK:]
        p_im = poles[0] * acc[ovl, BLOCK:] - acc[rows, BLOCK:] + poles[1] * acc[ovl, :BLOCK]
        out[0, rows] = (mask * (weights[0] * p_re - weights[1] * p_im)).astype(jnp.bfloat16)
        out[1, rows] = (-mask * (weights[0] * p_im + weights[1] * p_re)).astype(jnp.bfloat16)


def place_blocks(place, source, lines, core, blocks, copy=None):
    @pl.loop(0, 4 * len(lines))
    def _(entry):
        along = entry % 4
        across = sum(jnp.where(entry // 4 == n, second, 0) for n, second in enumerate(lines))
        y = (place[1] + jnp.where(core == 0, across, along)) % 4
        x = (place[2] + jnp.where(core == 0, along, across)) % 4
        step = (y * 2 + x // 2 - place[0] + 8) % 8
        slot = jnp.where(step > 4, 2 * (8 - step), jnp.maximum(2 * step - 1, 0))
        value = source[entry]
        blocks[slot, :, pl.ds(pl.multiple_of(((x % 2) * 2 + core) * 128, 128), 128)] = value
        if copy is not None:
            copy[entry] = value


def product_near(place, near, ahead, behind, blocks, joined):
    for k, (source, second) in enumerate(((near, 0), (ahead, 1), (behind, 3))):
        place_blocks(place, source, (second,), place[3], blocks, joined.at[4 * k : 4 * k + 4])


def product_far(place, before, opposite, partner, blocks):
    place_blocks(place, opposite, (2,), place[3], blocks)
    place_blocks(place, partner, (0, 1, 3), 1 - place[3], blocks)


def product_left(place, poles, weights, keep, before, partner, *rest):
    pieces, (out, blocks, held, acc, sems) = rest[:16], rest[16:]
    for i in range(8):
        for rel in range(2):
            pltpu.make_async_copy(pieces[2 * i + rel], held.at[i, rel], sems.at[i]).start()
    place_blocks(place, partner, (2,), 1 - place[3], blocks)

    def ready(i):
        pltpu.make_async_copy(held.at[i], held.at[i], sems.at[i]).wait()

    half_product(0, place, poles, weights, keep, blocks, ready, held, out, acc)


def product_right(place, poles, weights, keep, blocks, held, out, acc):
    half_product(1, place, poles, weights, keep, blocks, lambda i: None, held, out, acc)


def refined_sum(left, pieces):
    lhs = jnp.concatenate([left[:, part].reshape(512, 512) for part in range(2)], axis=1)
    rhs = [jnp.concatenate([pieces[side][part] for side in range(2)], axis=1) for part in range(2)]
    return DOT(lhs, jnp.concatenate(rhs))


def refine_pre(place, *rest):
    lines, pieces = rest[:4], rest[4 : 4 + 2 * PRE]
    acc, left, held, sems = rest[4 + 2 * PRE :]
    for i in range(PRE):
        for side in range(2):
            pltpu.make_async_copy(pieces[2 * i + side], held.at[i, side], sems.at[i, 0]).start()

    @pl.loop(0, 16)
    def _(k):
        i, half = k // 2, k % 2
        step = jnp.where(i % 2 == 1, (i + 1) // 2, (8 - i // 2) % 8)
        second, first = block_offsets(place, (place[0] + step) % 8, half, place[3])
        for n, line in enumerate(lines):

            @pl.when(second == n)
            def _():
                pltpu.make_async_copy(line.at[first], left.at[i, half], sems.at[i, 1]).start()

    acc[...] = jnp.zeros_like(acc)

    @pl.loop(0, PRE)
    def _(i):
        pltpu.make_async_copy(left.at[i], left.at[i], sems.at[i, 1]).wait()
        pltpu.make_async_copy(held.at[i], held.at[i], sems.at[i, 0]).wait()
        acc[...] += refined_sum(left.at[i], held.at[i])

    @pl.loop(PRE, 8)
    def _(i):
        pltpu.make_async_copy(left.at[i], left.at[i], sems.at[i, 1]).wait()


def refine_late(place, weights, keep, before, left, own, other, *rest):
    pieces, kept, away, acc = rest[:2], rest[2], rest[3], rest[4]
    acc[...] = before[...] + refined_sum(left.at[PRE], pieces)
    x_lo, kappa = place[2] % 2, place[1] * 4 + place[2]
    for slot, g in enumerate((own, other)):
        for out, core in ((kept, place[3]), (away, 1 - place[3])):
            tile = ((x_lo + slot) % 2) * 2 + core
            for j in range(2):
                mask = keep[place[0] * 4 + tile, kappa * 2 + j].astype(jnp.float32)
                cols, local = pl.ds(j * BLOCK, BLOCK), pl.ds(pl.multiple_of(core * BLOCK, BLOCK), BLOCK)
                own_re, own_im = [g[part, local, cols].astype(jnp.float32) for part in range(2)]
                twice = 2.0 * (weights[0] * own_re - weights[1] * own_im)
                out[slot, :, cols] = mask * (twice - acc[pl.ds(pl.multiple_of(tile * BLOCK, BLOCK), BLOCK), cols])


def call(kernel, outs, share, scalars=(), anywhere=(), vectors=(), scratch=(), room=10, aliases={}):
    smem, vmem = [pl.BlockSpec(memory_space=space) for space in (pltpu.SMEM, pltpu.VMEM)]
    return pl.pallas_call(
        kernel,
        out_shape=[jax.ShapeDtypeStruct(*out) for out in outs],
        in_specs=[smem] * len(scalars) + [pl.BlockSpec(memory_space=pl.ANY)] * len(anywhere) + [vmem] * len(vectors),
        out_specs=[vmem] * len(outs),
        scratch_shapes=scratch,
        input_output_aliases=aliases,
        compiler_params=pltpu.CompilerParams(vmem_limit_bytes=room << 20),
        cost_estimate=pl.CostEstimate(flops=share << 29, bytes_accessed=share << 21, transcendentals=0),
    )(*scalars, *anywhere, *vectors)


def per_device(hamilton, intersection, guess, poles, weights, keep):
    pole, z = lax.axis_index("pole"), lax.axis_index("z")
    y, x_hi, x_lo = lax.axis_index("row"), lax.axis_index("col"), lax.axis_index("x_lo")
    place = jnp.stack([z, y, x_hi * 2 + x_lo, pole]).astype(jnp.int32)
    w, keep, g = weights[0], keep[0], guess[0]
    f32, bf16 = jnp.float32, jnp.bfloat16

    shared = jnp.stack([lax.dynamic_slice_in_dim(a, pole * 128, 128, axis=0) for a in (hamilton, intersection)])
    ring = [shared] + [across_plane(shared, 1, d) for d in (1, 2, 3)]
    line = jnp.stack(ring)
    own = lax.dynamic_slice_in_dim(g, x_lo * 256, 256, axis=2)
    other = x_partner(lax.dynamic_slice_in_dim(g, (1 - x_lo) * 256, 256, axis=2))
    near = second_ring(line)
    chains = (line_gather(own, "u"), line_gather(other, "d"))
    pieces = [chain[step] for step in STEPS for chain in chains]
    guess_line = jnp.stack([g] + [across_plane(g, 1, d) for d in (1, 2, 3)])
    guess_lines = second_ring(guess_line)

    blocks_shape, at = ((8, 2, 512, 512), bf16), [place, poles[0], w, keep]
    blocks, joined = call(
        product_near,
        [blocks_shape, ((12, 2, 128, 512), bf16)],
        1,
        [place],
        (),
        [near[0], near[1], near[3]],
    )
    far = [other_core(joined), other_core(near[2])]
    (blocks,) = call(product_far, [blocks_shape], 1, [place], (), [blocks, near[2], far[0]], aliases={1: 0})
    held_shape, half_shape = ((8, 2, 2, 256, 256), bf16), ((2, 512, 128), bf16)
    halves = [None, None]
    halves[0], blocks, held = call(
        product_left,
        [half_shape, blocks_shape, held_shape],
        4,
        at,
        (),
        [blocks, far[1]] + pieces,
        [pltpu.VMEM((1024, 256), f32), pltpu.SemaphoreType.DMA((8,))],
        room=14,
        aliases={4: 1},
    )
    acc = pltpu.VMEM((1024, 256), f32)
    (halves[1],) = call(product_right, [half_shape], 4, at, (), [blocks, held], [acc])
    chains = (line_gather(halves[0], "u"), line_gather(halves[1], "d"))
    pieces = [chain[step] for step in STEPS for chain in chains]
    acc, left = call(
        refine_pre,
        [((512, 256), f32), ((8, 2, 2, 256, 512), bf16)],
        PRE,
        [place],
        (),
        guess_lines + pieces[: 2 * PRE],
        scratch=[
            pltpu.VMEM((PRE, 2, 2, 512, 128), bf16),
            pltpu.SemaphoreType.DMA((8, 2)),
        ],
        room=16,
    )
    kept, away = call(
        refine_late,
        [((2, 128, 256), f32)] * 2,
        1,
        [place, w, keep],
        (),
        [acc, left, own, other, *pieces[-2:]],
        [pltpu.VMEM((512, 256), f32)],
    )
    summed = kept + other_core(away)
    mine, theirs = summed[0], x_partner(summed[1])
    density = jnp.concatenate([jnp.where(x_lo == 0, mine, theirs), jnp.where(x_lo == 0, theirs, mine)], axis=1)
    return density.reshape(1, 1, 128, 512)


def solution(mesh):
    split = Mesh(mesh.devices.reshape(SIZES), ALL)
    return jax.shard_map(
        per_device,
        mesh=split,
        in_specs=(
            P(LAYER, ("row", "col")),
            P(LAYER, ("row", "col")),
            P("pole", None, LAYER, ("row", "col")),
            P("pole", None),
            P("pole", None),
            P("pole", None, None),
        ),
        out_specs=P(LAYER, "pole", None, ("row", "col")),
        check_vma=False,
    )
```
